32 devices in a mesh: pts: 16 (over z, x, core), dom: 2 (over y).
Axes of the slice: x: 2, y: 2, z: 4, core: 2. Of those that a mesh axis runs over, the one named last changes fastest.
Arguments:
- vectors: bfloat16 [2, 4096, 768], P('dom', 'pts'), may hold values from -6 to 6
- neighbor_shards: int32 [2, 4096, 1], P('dom', 'pts'), may hold values from 0 to 15, as said below
- neighbor_locals: int32 [2, 4096, 32], P('dom', 'pts'), may hold values from 0 to 255
- partition: int32 [2, 4096], P('dom', 'pts'), may hold values from 0 to 1, as said below
Outputs:
- moved_vectors: bfloat16 [2, 4096, 768], P('dom', 'pts')
- moved_reverse: bfloat16 [2, 4096, 32], P('dom', 'pts')
- moved_join: bfloat16 [2, 4096, 32], P('dom', 'pts')
The draws below stay inside these ranges and needn't reach their ends.
Inputs may be any that keep to these rules, and one draw needn't show every extreme that they name: `neighbor_shards`: the 1 numbers of one row are distinct, and the rows of one device come in aligned runs of 8 rows with equal numbers. Among the 256 rows of one device no number appears in more than 32 rows, and one number appears in exactly 32 rows. `partition`: for each id range, the 512 points of that range over all domains are split into 2 partitions of exactly 256 points each.
All inputs are finite; a program needn't handle non-finite values.
Results may differ from the reference program's by a relative error of at most 0.001.
Values may be sent and summed in bfloat16 or wider, within the bound.
A program may use at most 64 MiB of HBM per device.

```python
import jax
import jax.numpy as jnp
import numpy as np
from jax import lax

D = 768
K = 32
R = 32
P_DEV = 256
W = 1
CAP = 32
GRP = 8
DOMS = 2
NP = 4096
N_PTS = 16


def draw_partition(key, part):
    base_key = jax.random.fold_in(key, 11)
    key_stay, key_other, key_jitter = jax.random.split(base_key, 3)
    grid_shape = (DOMS, N_PTS, P_DEV)
    stay_flag = jax.random.randint(key_stay, grid_shape, 0, 2)
    other_dom = jax.random.randint(key_other, grid_shape, 0, DOMS)
    dom_index = jnp.arange(DOMS, dtype=jnp.int32)[:, None, None]
    preferred = jnp.where(stay_flag == 1, dom_index, other_dom)
    jitter = jax.random.randint(key_jitter, grid_shape, 0, 4096)
    local_ids = dom_index * P_DEV + jnp.arange(P_DEV, dtype=jnp.int32)[None, None, :]
    scores = (preferred * 4096 + jitter) * (DOMS * P_DEV) + local_ids
    columns = jnp.transpose(scores, (1, 0, 2)).reshape(N_PTS, DOMS * P_DEV)
    ranking = jnp.argsort(jnp.argsort(columns, axis=1), axis=1)
    parts = (ranking // P_DEV).reshape(N_PTS, DOMS, P_DEV)
    return jnp.transpose(parts, (1, 0, 2)).reshape(DOMS, N_PTS * P_DEV).astype(jnp.int32)


def draw_neighbor_shards(key, part):
    base_key = jax.random.fold_in(key, 23)
    key_raw, key_bias, key_fixed, key_cells = jax.random.split(base_key, 4)
    layer_count = CAP // GRP
    half_count = N_PTS // 2
    target_ids = jnp.arange(N_PTS, dtype=jnp.int32)
    raw_scores = jax.random.randint(key_raw, (DOMS, N_PTS, layer_count, N_PTS), 0, 1 << 20)
    bias_level = jax.random.randint(key_bias, (DOMS, 1, 1, N_PTS), 0, 4) * (1 << 18)
    scores = (raw_scores + bias_level) * N_PTS + target_ids[None, None, None, :]
    fixed_target = jax.random.randint(key_fixed, (DOMS, N_PTS, 1, 1), 0, N_PTS)
    scores = jnp.where(target_ids[None, None, None, :] == fixed_target, -1, scores)
    chosen = jnp.argsort(scores, axis=-1)[..., :half_count].astype(jnp.int32)
    cell_count = layer_count * half_count // W
    cells = chosen.reshape(DOMS, N_PTS, cell_count, W)
    cell_scores = jax.random.randint(key_cells, (DOMS, N_PTS, cell_count), 0, 1 << 20) * cell_count + jnp.arange(cell_count, dtype=jnp.int32)[None, None, :]
    cell_order = jnp.argsort(cell_scores, axis=-1).astype(jnp.int32)
    cells = jnp.take_along_axis(cells, cell_order[..., None], axis=2)
    rows = jnp.repeat(cells, GRP, axis=2)
    return rows.reshape(DOMS, NP, W).astype(jnp.int32)


def draw_vectors(key, part):
    base_key = jax.random.fold_in(key, 31)
    key_signs, key_noise = jax.random.split(base_key)
    signs = (2 * jax.random.randint(key_signs, (DOMS, 1, D), 0, 2) - 1).astype(jnp.float32)
    local_ids = jnp.arange(NP, dtype=jnp.int32) % P_DEV
    close_rows = local_ids % (4 * GRP) == 0
    along = jnp.where(close_rows, 0.75, 0.35).astype(jnp.float32)[None, :, None]
    across = jnp.sqrt(1.0 - along * along)
    noise = jax.random.truncated_normal(key_noise, -4.0, 4.0, (DOMS, NP, D), jnp.float32)
    return (along * signs + across * noise).astype(jnp.bfloat16)


def plant(array, rng, least, largest):
    longest = array.shape.index(max(array.shape))
    spots = []
    for shift in (0, 1):
        where = [jax.random.randint(jax.random.fold_in(rng, axis), (), 0, length) for axis, length in enumerate(array.shape)]
        where[longest] = (where[longest] + shift) % array.shape[longest]
        spots.append(tuple(where))
    return array.at[spots[0]].set(least).at[spots[1]].set(largest)


def setup_inputs(seed: int = 0) -> dict:
    keys = jax.random.split(jax.random.key(seed), 5)
    return {
        "vectors": draw_vectors(jax.random.fold_in(keys[4], 71), 0),
        "neighbor_shards": draw_neighbor_shards(jax.random.fold_in(keys[4], 71), 0),
        "neighbor_locals": plant(jax.random.randint(keys[2], (DOMS, NP, K), 0, P_DEV), jax.random.fold_in(keys[2], 1), 0, P_DEV - 1).astype(jnp.int32),
        "partition": draw_partition(jax.random.fold_in(keys[4], 71), 0),
    }


BIG_VALUE = 1.0e9


def smallest_rows(distance, allowed):
    masked = jnp.where(allowed, distance, BIG_VALUE)
    lowest = -lax.top_k(-masked, R)[0]
    return jnp.where(lowest < 0.5 * BIG_VALUE, lowest, 0.0)


def regroup(values, order_cols):
    feature = values.shape[-1]
    columns = values.reshape(DOMS, N_PTS, P_DEV, feature).transpose(1, 0, 2, 3).reshape(N_PTS, DOMS * P_DEV, feature)
    taken = jnp.take_along_axis(columns, order_cols[:, :, None], axis=1)
    return taken.reshape(N_PTS, DOMS, P_DEV, feature).transpose(1, 0, 2, 3).reshape(DOMS, N_PTS * P_DEV, feature)


def reference(vectors, neighbor_shards, neighbor_locals, partition):
    cap_rows = N_PTS * CAP
    sq_norms = jnp.sum(jnp.square(vectors.astype(jnp.float32)), axis=-1)
    per_slot = neighbor_shards[:, :, np.arange(K) % W]
    global_nbr = (per_slot * P_DEV + neighbor_locals).astype(jnp.int32)

    def one_shard(shard_num):
        domain = shard_num // N_PTS
        column = shard_num % N_PTS
        dom_vec = lax.dynamic_index_in_dim(vectors, domain, 0, keepdims=False)
        dom_norm = lax.dynamic_index_in_dim(sq_norms, domain, 0, keepdims=False)
        dom_shards = lax.dynamic_index_in_dim(neighbor_shards, domain, 0, keepdims=False)
        dom_nbr = lax.dynamic_index_in_dim(global_nbr, domain, 0, keepdims=False)
        member = jnp.any(dom_shards == column, axis=1)
        picked = jnp.argsort(1 - member.astype(jnp.int32), stable=True)[:cap_rows].astype(jnp.int32)
        is_valid = member[picked]
        row_start = (column * P_DEV).astype(jnp.int32)
        own_vec = lax.dynamic_slice_in_dim(dom_vec, row_start, P_DEV, 0)
        own_norm = lax.dynamic_slice_in_dim(dom_norm, row_start, P_DEV, 0)
        inner_prod = jnp.dot(own_vec, dom_vec[picked].T, preferred_element_type=jnp.float32)
        distance = (own_norm[:, None] + dom_norm[picked][None, :] - 2.0 * inner_prod) / D
        own_ids = row_start + jnp.arange(P_DEV, dtype=jnp.int32)
        join_ok = is_valid[None, :] & (picked[None, :] != own_ids[:, None])
        listed = jnp.any(dom_nbr[picked][None, :, :] == own_ids[:, None, None], axis=-1)
        return smallest_rows(distance, join_ok & listed), smallest_rows(distance, join_ok)

    reverse_rows, join_rows = lax.map(one_shard, jnp.arange(DOMS * N_PTS, dtype=jnp.int32))
    reverse_rows = reverse_rows.reshape(DOMS, NP, R).astype(jnp.bfloat16)
    join_rows = join_rows.reshape(DOMS, NP, R).astype(jnp.bfloat16)
    part_cols = partition.reshape(DOMS, N_PTS, P_DEV).transpose(1, 0, 2).reshape(N_PTS, DOMS * P_DEV)
    order_cols = jnp.argsort(part_cols, axis=1, stable=True).astype(jnp.int32)
    return (regroup(vectors, order_cols), regroup(reverse_rows, order_cols), regroup(join_rows, order_cols))
```

```python
import functools

import jax
import jax.numpy as jnp
from jax import lax
from jax.experimental import pallas as pl
from jax.experimental.pallas import tpu as pltpu
from jax.sharding import PartitionSpec as P

R = 32
BIG = 1.0e9
NT = (((1,), (1,)), ((), ()))
SHIFT = 1024


def oddeven_pairs(count):
    pairs = []

    def merge(lo, hi, r):
        step = r * 2
        if step < hi - lo:
            merge(lo, hi, step)
            merge(lo + r, hi, step)
            pairs.extend((i, i + r) for i in range(lo + r, hi - r, step))
        else:
            pairs.append((lo, lo + r))

    def sort(lo, hi):
        if hi - lo >= 1:
            mid = lo + (hi - lo) // 2
            sort(lo, mid)
            sort(mid + 1, hi)
            merge(lo, hi, 1)

    sort(0, count - 1)
    return pairs


PAIRS = oddeven_pairs(R)


def exchange(items, i, j):
    a, b = items[i], items[j]
    items[i], items[j] = jnp.minimum(a, b), jnp.maximum(a, b)


def sort_list(items):
    items = list(items)
    for i, j in PAIRS:
        exchange(items, i, j)
    return items


def merge_low(first, second):
    items = [jnp.minimum(first[i], second[R - 1 - i]) for i in range(R)]
    half = R // 2
    while half:
        for i in range(R):
            if not i & half:
                exchange(items, i, i + half)
        half //= 2
    return items


def dot(a, b):
    return jnp.dot(a, b, preferred_element_type=jnp.float32)


def dot_nt(a, b):
    return lax.dot_general(a, b, NT, preferred_element_type=jnp.float32)


def iota(shape, dim):
    return lax.broadcasted_iota(jnp.int32, shape, dim)


def onehot(cond):
    return jnp.where(cond, 1.0, 0.0).astype(jnp.bfloat16)


def kernel(n, doms, cap, *refs):
    refs = list(refs)
    vec, shards_t, locs, part = refs[:4]
    refs = refs[4:]
    wide = shards_t.shape[0] > 1
    slot_shard = refs.pop(0) if wide else None
    out_vec, out_rev, out_join = refs[:3]
    (sbuf, sinfo, rvec, rinfo, dvec, dpart, posn, ltile, lshard, onorm, dist, lists, rows, srows, drows,
     vs_sem, vr_sem, is_sem, ir_sem, ds_sem, dr_sem, ps_sem, pr_sem, rs_sem, rr_sem) = refs[3:]
    per, depth = vec.shape
    list_len = locs.shape[1]
    groups = cap // 8
    lanes = groups * list_len
    me = lax.axis_index("pts")
    dom = lax.axis_index("dom")
    bar = pltpu.get_barrier_semaphore()

    def greet_pts(o, carry):
        pl.semaphore_signal(bar, inc=1, device_id={"pts": lax.rem(me + o, n)}, device_id_type=pl.DeviceIdType.MESH)
        return carry

    def greet_dom(o, carry):
        pl.semaphore_signal(bar, inc=1, device_id={"dom": lax.rem(dom + o, doms)}, device_id_type=pl.DeviceIdType.MESH)
        return carry

    lax.fori_loop(1, n, greet_pts, 0)
    lax.fori_loop(1, doms, greet_dom, 0)

    own = vec[...]
    upper = onehot(iota((per, per), 0) < iota((per, per), 1))
    targets = iota((n, per), 0)
    member = shards_t[0:1, :] == targets
    for w in range(1, shards_t.shape[0]):
        member = member | (shards_t[w : w + 1, :] == targets)
    rank = dot(onehot(member), upper)
    posn[...] = jnp.where(member, rank, -1.0)
    tile = onehot(lax.rem(iota((list_len, lanes), 1), list_len) == iota((list_len, lanes), 0))
    ltile[...] = (dot(locs[...].astype(jnp.float32).astype(jnp.bfloat16), tile) + 1.0).astype(jnp.bfloat16)
    if wide:
        lshard[...] = dot(slot_shard[...].astype(jnp.float32).astype(jnp.bfloat16), tile)
    id_tile = (iota((per, lanes), 0) + 1).astype(jnp.float32).astype(jnp.bfloat16)
    lane_group = iota((8, lanes), 1) // list_len

    def pack(c, carry):
        row = posn[pl.ds(c, 1), :]
        pick = onehot(row == iota((cap, per), 0).astype(jnp.float32))
        sbuf[c] = dot(pick, own).astype(jnp.bfloat16)
        entry = ltile[...]
        if wide:
            entry = jnp.where(lshard[...] == c.astype(jnp.float32), entry.astype(jnp.float32), 0.0).astype(jnp.bfloat16)
        full = dot(pick, entry) + SHIFT * dot(pick, id_tile)
        flat = jnp.zeros((8, lanes), jnp.float32)
        for g in range(groups):
            flat = jnp.where(lane_group == g, full[8 * g : 8 * g + 8], flat)
        sinfo[c] = flat.astype(jnp.int32)
        return carry

    lax.fori_loop(0, n, pack, 0)
    square = jnp.square(own.astype(jnp.float32))
    high = square.astype(jnp.bfloat16)
    low = (square - high.astype(jnp.float32)).astype(jnp.bfloat16)
    ones = jnp.ones((8, depth), jnp.bfloat16)
    onorm[...] = dot_nt(ones, high) + dot_nt(ones, low)

    pl.semaphore_wait(bar, n - 1 + doms - 1)

    def vec_copy(c, slot_s, slot_r):
        return pltpu.make_async_remote_copy(
            src_ref=sbuf.at[c], dst_ref=rvec.at[slot_r], send_sem=vs_sem.at[slot_s], recv_sem=vr_sem.at[slot_r],
            device_id={"pts": c}, device_id_type=pl.DeviceIdType.MESH)

    def info_copy(c, slot_s, slot_r):
        return pltpu.make_async_remote_copy(
            src_ref=sinfo.at[c], dst_ref=rinfo.at[slot_r], send_sem=is_sem.at[slot_s], recv_sem=ir_sem.at[slot_r],
            device_id={"pts": c}, device_id_type=pl.DeviceIdType.MESH)

    def dom_copy(c, slot_r, src, dst, send, recv):
        return pltpu.make_async_remote_copy(
            src_ref=src, dst_ref=dst.at[slot_r], send_sem=send.at[c], recv_sem=recv.at[slot_r],
            device_id={"dom": c}, device_id_type=pl.DeviceIdType.MESH)

    def send_dom(o, carry):
        c = lax.rem(dom + o, doms)
        dom_copy(c, dom, part, dpart, ps_sem, pr_sem).start()
        dom_copy(c, dom, vec, dvec, ds_sem, dr_sem).start()
        return carry

    def send_pts(o, carry):
        c = lax.rem(me + o, n)
        info_copy(c, c, me).start()
        vec_copy(c, c, me).start()
        return carry

    lax.fori_loop(1, doms, send_dom, 0)
    lax.fori_loop(1, n, send_pts, 0)

    rvec[me] = sbuf[me]
    rinfo[me] = sinfo[me]
    dvec[dom] = own
    dpart[dom] = part[...]
    point = iota((8, per), 1) + 1

    def join(s, same):
        cand = rvec[s]
        wide_cand = cand.astype(jnp.float32)
        norm = jnp.sum(wide_cand * wide_cand, axis=1, keepdims=True)
        value = (onorm[0:1, :] + norm - 2.0 * dot_nt(cand, vec[...])) * (1.0 / depth)
        info = rinfo[s]
        ids = lax.div(info, SHIFT)
        entry = info - ids * SHIFT
        reverse, joined = [], []
        for g in range(groups):
            at = g * list_len
            listed = entry[:, at : at + 1] == point
            for k in range(1, list_len):
                listed = listed | (entry[:, at + k : at + k + 1] == point)
            slot_id = ids[:, at : at + 1]
            allowed = slot_id > 0
            if same:
                allowed = allowed & (slot_id != point)
            block = jnp.where(allowed, value[8 * g : 8 * g + 8], BIG)
            joined.append(block)
            reverse.append(jnp.where(listed, block, BIG))
        dist[0, s] = jnp.concatenate(reverse, axis=0).astype(jnp.bfloat16)
        dist[1, s] = jnp.concatenate(joined, axis=0).astype(jnp.bfloat16)

    join(me, True)

    def take(o, carry):
        s = lax.rem(me + n - o, n)
        info_copy(s, s, s).wait_recv()
        vec_copy(s, s, s).wait_recv()
        join(s, False)
        return carry

    def take_dom(o, carry):
        s = lax.rem(dom + doms - o, doms)
        dom_copy(s, s, part, dpart, ps_sem, pr_sem).wait_recv()
        dom_copy(s, s, vec, dvec, ds_sem, dr_sem).wait_recv()
        return carry

    def selections():
        base = jnp.zeros((8, 1), jnp.float32)
        for d in range(doms):
            here = jnp.broadcast_to(dpart[d], (8, per)) == dom
            flag = jnp.where(here, 1.0, 0.0)
            place = jnp.where(here, dot(flag.astype(jnp.bfloat16), upper) + base, -1.0)
            base = base + jnp.sum(flag, axis=1, keepdims=True)
            yield d, onehot(place[0:1, :] == iota((per, per), 0).astype(jnp.float32))

    half = n // 2
    lax.fori_loop(1, half, take, 0)
    lax.fori_loop(1, doms, take_dom, 0)
    total = jnp.zeros((per, depth), jnp.float32)
    for d, pick in selections():
        total = total + dot(pick, dvec[d])
    out_vec[...] = total.astype(jnp.bfloat16)
    lax.fori_loop(half, n, take, 0)

    blocks = cap // 16
    sources = R // blocks
    chunks = n // sources
    tiles = per // 128

    def sort_one(which, tile_id):
        columns = slice(tile_id * 128, tile_id * 128 + 128)

        def chunk(t):
            items = []
            for a in range(sources):
                for b in range(blocks):
                    items.append(dist[which, t * sources + a, 16 * b : 16 * b + 16, columns])
            items = [x.astype(jnp.float32) for x in sort_list(items)]
            return merge_low([x[:8] for x in items], [x[8:] for x in items])

        if chunks == 1:
            items = chunk(0)
            for i in range(R):
                lists[tile_id, i] = items[i]
        else:
            for i in range(R):
                lists[tile_id, i] = jnp.full((8, 128), BIG, jnp.float32)

            def more(t, carry):
                items = merge_low([lists[tile_id, i] for i in range(R)], chunk(t))
                for i in range(R):
                    lists[tile_id, i] = items[i]
                return carry

            lax.fori_loop(0, chunks, more, 0)

    upper_half = iota((8, 128), 0) < 4

    def both(which, carry):
        for tile_id in range(tiles):
            sort_one(which, tile_id)
        for pair in range(tiles // 2):
            first, second = [], []
            for i in range(R):
                a, b = lists[2 * pair, i], lists[2 * pair + 1, i]
                first.append(jnp.where(upper_half, a, b))
                second.append(pltpu.roll(jnp.where(upper_half, b, a), 4, 0))
            items = merge_low(first, second)
            for shift in (6, 7):
                items = merge_low(items, [pltpu.roll(x, shift, 0) for x in items])
            for i in range(R):
                x = jnp.where(items[i] < 0.5 * BIG, items[i], 0.0)
                rows[which, i : i + 1, 256 * pair : 256 * pair + 128] = x[0:1]
                rows[which, i : i + 1, 256 * pair + 128 : 256 * pair + 256] = x[4:5]
        srows[which] = rows[which].astype(jnp.bfloat16)
        return carry

    lax.fori_loop(0, 2, both, 0)

    def send_rows(o, carry):
        dom_copy(lax.rem(dom + o, doms), dom, srows, drows, rs_sem, rr_sem).start()
        return carry

    lax.fori_loop(1, doms, send_rows, 0)
    drows[dom] = srows[...]

    def take_rows(o, carry):
        s = lax.rem(dom + doms - o, doms)
        dom_copy(s, s, srows, drows, rs_sem, rr_sem).wait_recv()
        return carry

    lax.fori_loop(1, doms, take_rows, 0)
    total_rev = jnp.zeros((per, R), jnp.float32)
    total_join = jnp.zeros((per, R), jnp.float32)
    for d, pick in selections():
        total_rev = total_rev + dot_nt(pick, drows[d, 0])
        total_join = total_join + dot_nt(pick, drows[d, 1])
    out_rev[...] = total_rev.astype(jnp.bfloat16)
    out_join[...] = total_join.astype(jnp.bfloat16)

    def drain_pts(o, carry):
        c = lax.rem(me + o, n)
        info_copy(c, c, me).wait_send()
        vec_copy(c, c, me).wait_send()
        return carry

    def drain_dom(o, carry):
        c = lax.rem(dom + o, doms)
        dom_copy(c, dom, part, dpart, ps_sem, pr_sem).wait_send()
        dom_copy(c, dom, vec, dvec, ds_sem, dr_sem).wait_send()
        dom_copy(c, dom, srows, drows, rs_sem, rr_sem).wait_send()
        return carry

    lax.fori_loop(1, n, drain_pts, 0)
    lax.fori_loop(1, doms, drain_dom, 0)


def solution(mesh):
    n, doms = mesh.shape["pts"], mesh.shape["dom"]

    def per_device(vectors, neighbor_shards, neighbor_locals, partition):
        per, depth = vectors.shape[1:]
        width = neighbor_shards.shape[2]
        list_len = neighbor_locals.shape[2]
        cap = per // 8
        lanes = (cap // 8) * list_len
        operands = [vectors[0], neighbor_shards[0].T, neighbor_locals[0], partition]
        if width > 1:
            operands.append(neighbor_shards[0][:, jnp.arange(list_len) % width])
        bf16, f32, i32 = jnp.bfloat16, jnp.float32, jnp.int32
        dma = pltpu.SemaphoreType.DMA
        vmem = pl.BlockSpec(memory_space=pltpu.VMEM)
        out_vec, out_rev, out_join = pl.pallas_call(
            functools.partial(kernel, n, doms, cap),
            out_shape=(
                jax.ShapeDtypeStruct((per, depth), bf16),
                jax.ShapeDtypeStruct((per, R), bf16),
                jax.ShapeDtypeStruct((per, R), bf16),
            ),
            in_specs=[vmem] * len(operands),
            out_specs=(vmem, vmem, vmem),
            scratch_shapes=[
                pltpu.VMEM((n, cap, depth), bf16),
                pltpu.VMEM((n, 8, lanes), i32),
                pltpu.VMEM((n, cap, depth), bf16),
                pltpu.VMEM((n, 8, lanes), i32),
                pltpu.VMEM((doms, per, depth), bf16),
                pltpu.VMEM((doms, 1, per), i32),
                pltpu.VMEM((n, per), f32),
                pltpu.VMEM((per, lanes), bf16),
                pltpu.VMEM((per, lanes), f32),
                pltpu.VMEM((8, per), f32),
                pltpu.VMEM((2, n, cap, per), bf16),
                pltpu.VMEM((per // 128, R, 8, 128), f32),
                pltpu.VMEM((2, R, per), f32),
                pltpu.VMEM((2, R, per), bf16),
                pltpu.VMEM((doms, 2, R, per), bf16),
                dma((n,)), dma((n,)), dma((n,)), dma((n,)),
                dma((doms,)), dma((doms,)), dma((doms,)), dma((doms,)), dma((doms,)), dma((doms,)),
            ],
            compiler_params=pltpu.CompilerParams(collective_id=0, has_side_effects=True),
        )(*operands)
        return out_vec[None], out_rev[None], out_join[None]

    return jax.shard_map(
        per_device,
        mesh=mesh,
        in_specs=(
            P("dom", "pts", None),
            P("dom", "pts", None),
            P("dom", "pts", None),
            P("dom", "pts"),
        ),
        out_specs=(P("dom", "pts", None), P("dom", "pts", None), P("dom", "pts", None)),
        check_vma=False,
    )
```

```python
import functools

import jax
import jax.numpy as jnp
from jax import lax
from jax.experimental import pallas as pl
from jax.experimental.pallas import tpu as pltpu
from jax.sharding import PartitionSpec as P

R = 32
BIG = 1.0e9
NT = (((1,), (1,)), ((), ()))


def oddeven_pairs(count):
    pairs = []

    def merge(lo, hi, r):
        step = r * 2
        if step < hi - lo:
            merge(lo, hi, step)
            merge(lo + r, hi, step)
            pairs.extend((i, i + r) for i in range(lo + r, hi - r, step))
        else:
            pairs.append((lo, lo + r))

    def sort(lo, hi):
        if hi - lo >= 1:
            mid = lo + (hi - lo) // 2
            sort(lo, mid)
            sort(mid + 1, hi)
            merge(lo, hi, 1)

    sort(0, count - 1)
    return pairs


PAIRS = oddeven_pairs(R)


def exchange(items, i, j):
    a, b = items[i], items[j]
    items[i], items[j] = jnp.minimum(a, b), jnp.maximum(a, b)


def sort_list(items):
    items = list(items)
    for i, j in PAIRS:
        exchange(items, i, j)
    return items


def merge_low(first, second):
    items = [jnp.minimum(first[i], second[R - 1 - i]) for i in range(R)]
    half = R // 2
    while half:
        for i in range(R):
            if not i & half:
                exchange(items, i, i + half)
        half //= 2
    return items


def dot(a, b):
    return jnp.dot(a, b, preferred_element_type=jnp.float32)


def dot_nt(a, b):
    return lax.dot_general(a, b, NT, preferred_element_type=jnp.float32)


def iota(shape, dim):
    return lax.broadcasted_iota(jnp.int32, shape, dim)


def onehot(cond):
    return jnp.where(cond, 1.0, 0.0).astype(jnp.bfloat16)


def kernel(n, doms, cap, *refs):
    refs = list(refs)
    vec, shards_hbm, locs_hbm, part_hbm = refs[:4]
    refs = refs[4:]
    wide = shards_hbm.shape[0] > 1
    slot_shard_hbm = refs.pop(0) if wide else None
    out_vec, out_rows = refs[:2]
    (own_ref, shards_t, locs, part, slot_shard, sbuf, sinfo, rvec, rinfo, dvec, dpart, posn, ltile, lshard, selfid,
     onorm, dist, lists, rows, srows, drows,
     in_sem, vs_sem, vr_sem, is_sem, ir_sem, ds_sem, dr_sem, ps_sem, pr_sem, rs_sem, rr_sem) = refs[2:]
    per, depth = vec.shape
    list_len = locs.shape[0]
    groups = cap // 8
    lanes = groups * list_len
    me = lax.axis_index("pts")
    dom = lax.axis_index("dom")
    bar = pltpu.get_barrier_semaphore()
    fetches = [pltpu.make_async_copy(shards_hbm, shards_t, in_sem.at[0]),
               pltpu.make_async_copy(locs_hbm, locs, in_sem.at[1]),
               pltpu.make_async_copy(part_hbm, part, in_sem.at[2]),
               pltpu.make_async_copy(vec, own_ref, in_sem.at[3])]
    if wide:
        fetches.append(pltpu.make_async_copy(slot_shard_hbm, slot_shard, in_sem.at[4]))
    for fetch in fetches:
        fetch.start()

    def greet_pts(o, carry):
        pl.semaphore_signal(bar, inc=1, device_id={"pts": lax.rem(me + o, n)}, device_id_type=pl.DeviceIdType.MESH)
        return carry

    def greet_dom(o, carry):
        pl.semaphore_signal(bar, inc=1, device_id={"dom": lax.rem(dom + o, doms)}, device_id_type=pl.DeviceIdType.MESH)
        return carry

    lax.fori_loop(1, n, greet_pts, 0)
    lax.fori_loop(1, doms, greet_dom, 0)

    half = n // 2
    side = me // half
    local = lax.rem(me, half)

    def target(o):
        return lax.rem(side + 1 + o // half, 2) * half + lax.rem(local + o, half)

    def source(o):
        return lax.rem(side + 1 + o // half, 2) * half + lax.rem(local + half - lax.rem(o, half), half)

    order = [o for o in range(half + 1, n)] + [o for o in range(half)]

    for fetch in fetches:
        fetch.wait()
    own = own_ref[...]
    upper = onehot(iota((per, per), 0) < iota((per, per), 1))
    targets = iota((n, per), 0)
    member = shards_t[0:1, :] == targets
    for w in range(1, shards_t.shape[0]):
        member = member | (shards_t[w : w + 1, :] == targets)
    rank = dot(onehot(member), upper)
    posn[...] = jnp.where(member, rank, -1.0)
    tile = onehot(lax.rem(iota((list_len, lanes), 1), list_len) == iota((list_len, lanes), 0))

    def spread(ref):
        return lax.dot_general(ref[...].astype(jnp.float32).astype(jnp.bfloat16), tile, (((0,), (0,)), ((), ())),
                               preferred_element_type=jnp.float32)

    ltile[...] = (spread(locs) + 1.0).astype(jnp.bfloat16)
    if wide:
        lshard[...] = spread(slot_shard)
    lane_group = iota((8, lanes), 1) // list_len
    slot_row = iota((cap, per), 0).astype(jnp.float32)

    def fold(full):
        flat = jnp.zeros((8, lanes), jnp.float32)
        for g in range(groups):
            flat = jnp.where(lane_group == g, full[8 * g : 8 * g + 8], flat)
        return flat.astype(jnp.bfloat16)

    batch = 4

    def pack(b, carry):
        dests = [target(b * batch + t) for t in range(batch)]
        picks = [onehot(posn[pl.ds(c, 1), :] == slot_row) for c in dests]
        pick = jnp.concatenate(picks, axis=0)
        packed = dot(pick, own_ref[...]).astype(jnp.bfloat16)
        if not wide:
            full = dot(pick, ltile[...])
        for t, c in enumerate(dests):
            sbuf[c] = packed[t * cap : t * cap + cap]
            if wide:
                entry = jnp.where(lshard[...] == c.astype(jnp.float32), ltile[...].astype(jnp.float32), 0.0)
                sinfo[c] = fold(dot(picks[t], entry.astype(jnp.bfloat16)))
            else:
                sinfo[c] = fold(full[t * cap : t * cap + cap])
        return carry

    if n <= 16:
        for b in range(n // batch):
            pack(b, 0)
    else:
        lax.fori_loop(0, n // batch, pack, 0)

    pl.semaphore_wait(bar, n - 1 + doms - 1)

    def vec_copy(c, slot_s, slot_r):
        return pltpu.make_async_remote_copy(
            src_ref=sbuf.at[c], dst_ref=rvec.at[slot_r], send_sem=vs_sem.at[slot_s], recv_sem=vr_sem.at[slot_r],
            device_id={"pts": c}, device_id_type=pl.DeviceIdType.MESH)

    def info_copy(c, slot_s, slot_r):
        return pltpu.make_async_remote_copy(
            src_ref=sinfo.at[c], dst_ref=rinfo.at[slot_r], send_sem=is_sem.at[slot_s], recv_sem=ir_sem.at[slot_r],
            device_id={"pts": c}, device_id_type=pl.DeviceIdType.MESH)

    def dom_copy(c, slot_r, src, dst, send, recv):
        return pltpu.make_async_remote_copy(
            src_ref=src, dst_ref=dst.at[slot_r], send_sem=send.at[c], recv_sem=recv.at[slot_r],
            device_id={"dom": c}, device_id_type=pl.DeviceIdType.MESH)

    def send_dom(o, carry):
        c = lax.rem(dom + o, doms)
        dom_copy(c, dom, part, dpart, ps_sem, pr_sem).start()
        dom_copy(c, dom, own_ref, dvec, ds_sem, dr_sem).start()
        return carry

    for o in order:
        c = target(o)
        info_copy(c, c, me).start()
        vec_copy(c, c, me).start()
    lax.fori_loop(1, doms, send_dom, 0)

    square = jnp.square(own.astype(jnp.float32))
    high = square.astype(jnp.bfloat16)
    low = (square - high.astype(jnp.float32)).astype(jnp.bfloat16)
    ones = jnp.ones((8, depth), jnp.bfloat16)
    onorm[...] = dot_nt(ones, high) + dot_nt(ones, low)
    id_tile = (iota((per, 128), 0) + 1).astype(jnp.float32).astype(jnp.bfloat16)
    selfid[...] = dot(onehot(posn[pl.ds(me, 1), :] == slot_row), id_tile)
    rvec[me] = sbuf[me]
    rinfo[me] = sinfo[me]
    dvec[dom] = own
    dpart[dom] = part[...]
    point = (iota((8, per), 1) + 1).astype(jnp.float32)
    width = shards_t.shape[0]

    def join(s, same):
        cand = rvec[s]
        wide_cand = cand.astype(jnp.float32)
        norm = jnp.sum(wide_cand * wide_cand, axis=1, keepdims=True)
        value = (onorm[0:1, :] + norm - 2.0 * dot_nt(cand, own_ref[...])) * (1.0 / depth)
        entry = rinfo[s].astype(jnp.float32)
        reverse, joined = [], []
        for g in range(groups):
            at = g * list_len
            listed = entry[:, at : at + 1] == point
            for k in range(1, list_len):
                listed = listed | (entry[:, at + k : at + k + 1] == point)
            allowed = entry[:, at : at + 1] > 0.0
            for w in range(1, width):
                allowed = allowed | (entry[:, at + w : at + w + 1] > 0.0)
            if same:
                allowed = allowed & (selfid[8 * g : 8 * g + 8, 0:1] != point)
            block = jnp.where(allowed, value[8 * g : 8 * g + 8], BIG)
            joined.append(block)
            reverse.append(jnp.where(listed, block, BIG))
        dist[0, s] = jnp.concatenate(reverse, axis=0).astype(jnp.bfloat16)
        dist[1, s] = jnp.concatenate(joined, axis=0).astype(jnp.bfloat16)

    join(me, True)

    def take(o, carry):
        s = source(lax.rem(o + half, n))
        info_copy(s, s, s).wait_recv()
        vec_copy(s, s, s).wait_recv()
        join(s, False)
        return carry

    def take_dom(o, carry):
        s = lax.rem(dom + doms - o, doms)
        dom_copy(s, s, part, dpart, ps_sem, pr_sem).wait_recv()
        dom_copy(s, s, own_ref, dvec, ds_sem, dr_sem).wait_recv()
        return carry

    def selections():
        base = jnp.zeros((8, 1), jnp.float32)
        for d in range(doms):
            here = jnp.broadcast_to(dpart[d], (8, per)) == dom
            flag = jnp.where(here, 1.0, 0.0)
            place = jnp.where(here, dot(flag.astype(jnp.bfloat16), upper) + base, -1.0)
            base = base + jnp.sum(flag, axis=1, keepdims=True)
            yield d, onehot(place[0:1, :] == iota((per, per), 0).astype(jnp.float32))

    lax.fori_loop(1, half, take, 0)
    lax.fori_loop(1, doms, take_dom, 0)
    total = jnp.zeros((per, depth), jnp.float32)
    for d, pick in selections():
        total = total + dot(pick, dvec[d])
    out_vec[...] = total.astype(jnp.bfloat16)
    lax.fori_loop(half, n, take, 0)

    blocks = cap // 16
    sources = R // blocks
    chunks = n // sources
    tiles = per // 128

    def sort_one(which, tile_id):
        columns = slice(tile_id * 128, tile_id * 128 + 128)

        def chunk(t):
            items = []
            for a in range(sources):
                for b in range(blocks):
                    items.append(dist[which, t * sources + a, 16 * b : 16 * b + 16, columns])
            items = [x.astype(jnp.float32) for x in sort_list(items)]
            return merge_low([x[:8] for x in items], [x[8:] for x in items])

        if chunks == 1:
            items = chunk(0)
            for i in range(R):
                lists[tile_id, i] = items[i]
        else:
            for i in range(R):
                lists[tile_id, i] = jnp.full((8, 128), BIG, jnp.float32)

            def more(t, carry):
                items = merge_low([lists[tile_id, i] for i in range(R)], chunk(t))
                for i in range(R):
                    lists[tile_id, i] = items[i]
                return carry

            lax.fori_loop(0, chunks, more, 0)

    upper_half = iota((8, 128), 0) < 4

    def both(which, carry):
        for tile_id in range(tiles):
            sort_one(which, tile_id)
        for pair in range(tiles // 2):
            first, second = [], []
            for i in range(R):
                a, b = lists[2 * pair, i], lists[2 * pair + 1, i]
                first.append(jnp.where(upper_half, a, b))
                second.append(pltpu.roll(jnp.where(upper_half, b, a), 4, 0))
            items = merge_low(first, second)
            for shift in (6, 7):
                items = merge_low(items, [pltpu.roll(x, shift, 0) for x in items])
            for i in range(R):
                x = jnp.where(items[i] < 0.5 * BIG, items[i], 0.0)
                rows[which, i : i + 1, 256 * pair : 256 * pair + 128] = x[0:1]
                rows[which, i : i + 1, 256 * pair + 128 : 256 * pair + 256] = x[4:5]
        srows[which] = rows[which].astype(jnp.bfloat16)
        return carry

    def rows_copy(c, slot_r, which):
        return pltpu.make_async_remote_copy(
            src_ref=srows.at[which], dst_ref=drows.at[slot_r, which], send_sem=rs_sem.at[which, c],
            recv_sem=rr_sem.at[which, slot_r], device_id={"dom": c}, device_id_type=pl.DeviceIdType.MESH)

    for which in range(2):
        both(which, 0)

        def send_rows(o, carry):
            rows_copy(lax.rem(dom + o, doms), dom, which).start()
            return carry

        lax.fori_loop(1, doms, send_rows, 0)
    drows[dom] = srows[...]

    def take_rows(o, carry):
        s = lax.rem(dom + doms - o, doms)
        rows_copy(s, s, 0).wait_recv()
        rows_copy(s, s, 1).wait_recv()
        return carry

    lax.fori_loop(1, doms, take_rows, 0)
    moved = jnp.zeros((2 * R, per), jnp.float32)
    for d, pick in selections():
        moved = moved + dot_nt(jnp.concatenate([drows[d, 0], drows[d, 1]], axis=0), pick)
    out_rows[...] = moved.astype(jnp.bfloat16)

    def drain_pts(o, carry):
        c = lax.rem(me + o, n)
        info_copy(c, c, me).wait_send()
        vec_copy(c, c, me).wait_send()
        return carry

    def drain_dom(o, carry):
        c = lax.rem(dom + o, doms)
        dom_copy(c, dom, part, dpart, ps_sem, pr_sem).wait_send()
        dom_copy(c, dom, own_ref, dvec, ds_sem, dr_sem).wait_send()
        rows_copy(c, dom, 0).wait_send()
        rows_copy(c, dom, 1).wait_send()
        return carry

    lax.fori_loop(1, n, drain_pts, 0)
    lax.fori_loop(1, doms, drain_dom, 0)


def place(found_vec, found_rows, out_vec, out_rev, out_join):
    out_vec[...] = found_vec[...]
    out_rev[...] = found_rows[:R]
    out_join[...] = found_rows[R:]


def solution(mesh):
    n, doms = mesh.shape["pts"], mesh.shape["dom"]

    def per_device(vectors, neighbor_shards, neighbor_locals, partition):
        per, depth = vectors.shape[1:]
        width = neighbor_shards.shape[2]
        list_len = neighbor_locals.shape[2]
        cap = per // 8
        lanes = (cap // 8) * list_len
        operands = [vectors[0], neighbor_shards[0].T, neighbor_locals[0].T, partition]
        if width > 1:
            operands.append(neighbor_shards[0].T[jnp.arange(list_len) % width])
        bf16, f32, i32 = jnp.bfloat16, jnp.float32, jnp.int32
        dma = pltpu.SemaphoreType.DMA
        vmem = pl.BlockSpec(memory_space=pltpu.VMEM)
        anywhere = pl.BlockSpec(memory_space=pltpu.HBM)
        shapes = (jax.ShapeDtypeStruct((per, depth), bf16), jax.ShapeDtypeStruct((2 * R, per), bf16))
        found_vec, found_rows = pl.pallas_call(
            functools.partial(kernel, n, doms, cap),
            out_shape=shapes,
            in_specs=[anywhere] * len(operands),
            out_specs=(vmem, vmem),
            scratch_shapes=[
                pltpu.VMEM((per, depth), bf16),
                pltpu.VMEM((width, per), i32),
                pltpu.VMEM((list_len, per), i32),
                pltpu.VMEM((1, per), i32),
                pltpu.VMEM((list_len, per), i32),
                pltpu.VMEM((n, cap, depth), bf16),
                pltpu.VMEM((n, 8, lanes), bf16),
                pltpu.VMEM((n, cap, depth), bf16),
                pltpu.VMEM((n, 8, lanes), bf16),
                pltpu.VMEM((doms, per, depth), bf16),
                pltpu.VMEM((doms, 1, per), i32),
                pltpu.VMEM((n, per), f32),
                pltpu.VMEM((per, lanes), bf16),
                pltpu.VMEM((per, lanes), f32),
                pltpu.VMEM((cap, 128), f32),
                pltpu.VMEM((8, per), f32),
                pltpu.VMEM((2, n, cap, per), bf16),
                pltpu.VMEM((per // 128, R, 8, 128), f32),
                pltpu.VMEM((2, R, per), f32),
                pltpu.VMEM((2, R, per), bf16),
                pltpu.VMEM((doms, 2, R, per), bf16),
                dma((5,)),
                dma((n,)), dma((n,)), dma((n,)), dma((n,)),
                dma((doms,)), dma((doms,)), dma((doms,)), dma((doms,)), dma((2, doms)), dma((2, doms)),
            ],
            compiler_params=pltpu.CompilerParams(
                collective_id=0, has_side_effects=True, vmem_limit_bytes=32 * 1024 * 1024),
        )(*[pltpu.with_memory_space_constraint(x, pltpu.HBM) for x in operands])
        out_vec, out_rev, out_join = pl.pallas_call(
            place,
            out_shape=(shapes[0], jax.ShapeDtypeStruct((R, per), bf16), jax.ShapeDtypeStruct((R, per), bf16)),
            in_specs=[vmem, vmem],
            out_specs=(vmem, vmem, vmem),
            compiler_params=pltpu.CompilerParams(vmem_limit_bytes=8 * 1024 * 1024),
        )(found_vec, found_rows)
        return out_vec[None], out_rev.T[None], out_join.T[None]

    return jax.shard_map(
        per_device,
        mesh=mesh,
        in_specs=(
            P("dom", "pts", None),
            P("dom", "pts", None),
            P("dom", "pts", None),
            P("dom", "pts"),
        ),
        out_specs=(P("dom", "pts", None), P("dom", "pts", None), P("dom", "pts", None)),
        check_vma=False,
    )
```

```python
import functools

import jax
import jax.numpy as jnp
from jax import lax
from jax.experimental import pallas as pl
from jax.experimental.pallas import tpu as pltpu
from jax.sharding import PartitionSpec as P

R = 32
BIG = 1.0e9
NT = (((1,), (1,)), ((), ()))


def oddeven_pairs(count):
    pairs = []

    def merge(lo, hi, r):
        step = r * 2
        if step < hi - lo:
            merge(lo, hi, step)
            merge(lo + r, hi, step)
            pairs.extend((i, i + r) for i in range(lo + r, hi - r, step))
        else:
            pairs.append((lo, lo + r))

    def sort(lo, hi):
        if hi - lo >= 1:
            mid = lo + (hi - lo) // 2
            sort(lo, mid)
            sort(mid + 1, hi)
            merge(lo, hi, 1)

    sort(0, count - 1)
    return pairs


PAIRS = oddeven_pairs(R)


def exchange(items, i, j):
    a, b = items[i], items[j]
    items[i], items[j] = jnp.minimum(a, b), jnp.maximum(a, b)


def sort_list(items):
    items = list(items)
    for i, j in PAIRS:
        exchange(items, i, j)
    return items


def merge_low(first, second):
    items = [jnp.minimum(first[i], second[R - 1 - i]) for i in range(R)]
    half = R // 2
    while half:
        for i in range(R):
            if not i & half:
                exchange(items, i, i + half)
        half //= 2
    return items


def dot(a, b):
    return jnp.dot(a, b, preferred_element_type=jnp.float32)


def dot_nt(a, b):
    return lax.dot_general(a, b, NT, preferred_element_type=jnp.float32)


def iota(shape, dim):
    return lax.broadcasted_iota(jnp.int32, shape, dim)


def onehot(cond):
    return jnp.where(cond, 1.0, 0.0).astype(jnp.bfloat16)


def kernel(n, doms, cap, *refs):
    refs = list(refs)
    vec, shards_hbm, locs_hbm, part_hbm = refs[:4]
    refs = refs[4:]
    wide = shards_hbm.shape[0] > 1
    slot_shard_hbm = refs.pop(0) if wide else None
    out_vec, out_rows = refs[:2]
    (own_ref, shards_t, locs, part, slot_shard, sbuf, sinfo, rvec, rinfo, dvec, dpart, posn, ltile, lshard, selfid,
     onorm, dist, lists, rows, srows, drows,
     in_sem, vs_sem, vr_sem, is_sem, ir_sem, ds_sem, dr_sem, ps_sem, pr_sem, rs_sem, rr_sem) = refs[2:]
    per, depth = vec.shape
    list_len = locs.shape[0]
    groups = cap // 8
    lanes = groups * list_len
    me = lax.axis_index("pts")
    dom = lax.axis_index("dom")
    bar = pltpu.get_barrier_semaphore()
    fetches = [pltpu.make_async_copy(shards_hbm, shards_t, in_sem.at[0]),
               pltpu.make_async_copy(locs_hbm, locs, in_sem.at[1]),
               pltpu.make_async_copy(part_hbm, part, in_sem.at[2]),
               pltpu.make_async_copy(vec, own_ref, in_sem.at[3])]
    if wide:
        fetches.append(pltpu.make_async_copy(slot_shard_hbm, slot_shard, in_sem.at[4]))
    for fetch in fetches:
        fetch.start()

    def greet_pts(o, carry):
        pl.semaphore_signal(bar, inc=1, device_id={"pts": lax.rem(me + o, n)}, device_id_type=pl.DeviceIdType.MESH)
        return carry

    def greet_dom(o, carry):
        pl.semaphore_signal(bar, inc=1, device_id={"dom": lax.rem(dom + o, doms)}, device_id_type=pl.DeviceIdType.MESH)
        return carry

    lax.fori_loop(1, n, greet_pts, 0)
    lax.fori_loop(1, doms, greet_dom, 0)

    half = n // 2
    side = me // half
    local = lax.rem(me, half)

    def target(o):
        return lax.rem(side + 1 + o // half, 2) * half + lax.rem(local + o, half)

    def source(o):
        return lax.rem(side + 1 + o // half, 2) * half + lax.rem(local + half - lax.rem(o, half), half)

    order = [o for o in range(half + 1, n)] + [o * 3 % half for o in range(half)]

    for fetch in fetches:
        fetch.wait()
    own = own_ref[...]
    upper = onehot(iota((per, per), 0) < iota((per, per), 1))
    targets = iota((n, per), 0)
    member = shards_t[0:1, :] == targets
    for w in range(1, shards_t.shape[0]):
        member = member | (shards_t[w : w + 1, :] == targets)
    rank = dot(onehot(member), upper)
    posn[...] = jnp.where(member, rank, -1.0)
    tile = onehot(lax.rem(iota((list_len, lanes), 1), list_len) == iota((list_len, lanes), 0))

    def spread(ref):
        return lax.dot_general(ref[...].astype(jnp.float32).astype(jnp.bfloat16), tile, (((0,), (0,)), ((), ())),
                               preferred_element_type=jnp.float32)

    ltile[...] = (spread(locs) + 1.0).astype(jnp.bfloat16)
    if wide:
        lshard[...] = spread(slot_shard)
    lane_group = iota((8, lanes), 1) // list_len
    slot_row = iota((cap, per), 0).astype(jnp.float32)

    def fold(full):
        flat = jnp.zeros((8, lanes), jnp.float32)
        for g in range(groups):
            flat = jnp.where(lane_group == g, full[8 * g : 8 * g + 8], flat)
        return flat.astype(jnp.bfloat16)

    batch = 4

    def pack(b, carry):
        dests = [target(b * batch + t) for t in range(batch)]
        picks = [onehot(posn[pl.ds(c, 1), :] == slot_row) for c in dests]
        pick = jnp.concatenate(picks, axis=0)
        packed = dot(pick, own_ref[...]).astype(jnp.bfloat16)
        if not wide:
            full = dot(pick, ltile[...])
        for t, c in enumerate(dests):
            sbuf[c] = packed[t * cap : t * cap + cap]
            if wide:
                entry = jnp.where(lshard[...] == c.astype(jnp.float32), ltile[...].astype(jnp.float32), 0.0)
                sinfo[c] = fold(dot(picks[t], entry.astype(jnp.bfloat16)))
            else:
                sinfo[c] = fold(full[t * cap : t * cap + cap])
        return carry

    if n <= 16:
        for b in range(n // batch):
            pack(b, 0)
    else:
        lax.fori_loop(0, n // batch, pack, 0)

    pl.semaphore_wait(bar, n - 1 + doms - 1)

    def vec_copy(c, slot_s, slot_r):
        return pltpu.make_async_remote_copy(
            src_ref=sbuf.at[c], dst_ref=rvec.at[slot_r], send_sem=vs_sem.at[slot_s], recv_sem=vr_sem.at[slot_r],
            device_id={"pts": c}, device_id_type=pl.DeviceIdType.MESH)

    def info_copy(c, slot_s, slot_r):
        return pltpu.make_async_remote_copy(
            src_ref=sinfo.at[c], dst_ref=rinfo.at[slot_r], send_sem=is_sem.at[slot_s], recv_sem=ir_sem.at[slot_r],
            device_id={"pts": c}, device_id_type=pl.DeviceIdType.MESH)

    def dom_copy(c, slot_r, src, dst, send, recv):
        return pltpu.make_async_remote_copy(
            src_ref=src, dst_ref=dst.at[slot_r], send_sem=send.at[c], recv_sem=recv.at[slot_r],
            device_id={"dom": c}, device_id_type=pl.DeviceIdType.MESH)

    def send_dom(o, carry):
        c = lax.rem(dom + o, doms)
        dom_copy(c, dom, part, dpart, ps_sem, pr_sem).start()
        dom_copy(c, dom, own_ref, dvec, ds_sem, dr_sem).start()
        return carry

    for o in order:
        c = target(o)
        info_copy(c, c, me).start()
        vec_copy(c, c, me).start()
    lax.fori_loop(1, doms, send_dom, 0)

    square = jnp.square(own.astype(jnp.float32))
    high = square.astype(jnp.bfloat16)
    low = (square - high.astype(jnp.float32)).astype(jnp.bfloat16)
    ones = jnp.ones((8, depth), jnp.bfloat16)
    onorm[...] = dot_nt(ones, high) + dot_nt(ones, low)
    id_tile = (iota((per, 128), 0) + 1).astype(jnp.float32).astype(jnp.bfloat16)
    selfid[...] = dot(onehot(posn[pl.ds(me, 1), :] == slot_row), id_tile)
    rvec[me] = sbuf[me]
    rinfo[me] = sinfo[me]
    dvec[dom] = own
    dpart[dom] = part[...]
    point = (iota((8, per), 1) + 1).astype(jnp.float32)
    width = shards_t.shape[0]

    def join(s, same):
        cand = rvec[s]
        wide_cand = cand.astype(jnp.float32)
        norm = jnp.sum(wide_cand * wide_cand, axis=1, keepdims=True)
        value = (onorm[0:1, :] + norm - 2.0 * dot_nt(cand, own_ref[...])) * (1.0 / depth)
        entry = rinfo[s].astype(jnp.float32)
        reverse, joined = [], []
        for g in range(groups):
            at = g * list_len
            listed = entry[:, at : at + 1] == point
            for k in range(1, list_len):
                listed = listed | (entry[:, at + k : at + k + 1] == point)
            allowed = entry[:, at : at + 1] > 0.0
            for w in range(1, width):
                allowed = allowed | (entry[:, at + w : at + w + 1] > 0.0)
            if same:
                allowed = allowed & (selfid[8 * g : 8 * g + 8, 0:1] != point)
            block = jnp.where(allowed, value[8 * g : 8 * g + 8], BIG)
            joined.append(block)
            reverse.append(jnp.where(listed, block, BIG))
        dist[0, s] = jnp.concatenate(reverse, axis=0).astype(jnp.bfloat16)
        dist[1, s] = jnp.concatenate(joined, axis=0).astype(jnp.bfloat16)

    join(me, True)

    def take(o, carry, near=False):
        s = source(lax.rem(o + half, n) if near else lax.rem((o - half) * 3, half))
        info_copy(s, s, s).wait_recv()
        vec_copy(s, s, s).wait_recv()
        join(s, False)
        return carry

    def take_dom(o, carry):
        s = lax.rem(dom + doms - o, doms)
        dom_copy(s, s, part, dpart, ps_sem, pr_sem).wait_recv()
        dom_copy(s, s, own_ref, dvec, ds_sem, dr_sem).wait_recv()
        return carry

    def selections():
        base = jnp.zeros((8, 1), jnp.float32)
        for d in range(doms):
            here = jnp.broadcast_to(dpart[d], (8, per)) == dom
            flag = jnp.where(here, 1.0, 0.0)
            place = jnp.where(here, dot(flag.astype(jnp.bfloat16), upper) + base, -1.0)
            base = base + jnp.sum(flag, axis=1, keepdims=True)
            yield d, onehot(place[0:1, :] == iota((per, per), 0).astype(jnp.float32))

    lax.fori_loop(1, half, functools.partial(take, near=True), 0)
    lax.fori_loop(1, doms, take_dom, 0)
    total = jnp.zeros((per, depth), jnp.float32)
    for d, pick in selections():
        total = total + dot(pick, dvec[d])
    out_vec[...] = total.astype(jnp.bfloat16)
    lax.fori_loop(half, n, take, 0)

    blocks = cap // 16
    sources = R // blocks
    chunks = n // sources
    tiles = per // 128

    def sort_one(which, tile_id):
        columns = slice(tile_id * 128, tile_id * 128 + 128)

        def chunk(t):
            items = []
            for a in range(sources):
                for b in range(blocks):
                    items.append(dist[which, t * sources + a, 16 * b : 16 * b + 16, columns])
            items = [x.astype(jnp.float32) for x in sort_list(items)]
            return merge_low([x[:8] for x in items], [x[8:] for x in items])

        if chunks == 1:
            items = chunk(0)
            for i in range(R):
                lists[tile_id, i] = items[i]
        else:
            for i in range(R):
                lists[tile_id, i] = jnp.full((8, 128), BIG, jnp.float32)

            def more(t, carry):
                items = merge_low([lists[tile_id, i] for i in range(R)], chunk(t))
                for i in range(R):
                    lists[tile_id, i] = items[i]
                return carry

            lax.fori_loop(0, chunks, more, 0)

    upper_half = iota((8, 128), 0) < 4

    def both(which, carry):
        for tile_id in range(tiles):
            sort_one(which, tile_id)
        for pair in range(tiles // 2):
            first, second = [], []
            for i in range(R):
                a, b = lists[2 * pair, i], lists[2 * pair + 1, i]
                first.append(jnp.where(upper_half, a, b))
                second.append(pltpu.roll(jnp.where(upper_half, b, a), 4, 0))
            items = merge_low(first, second)
            for shift in (6, 7):
                items = merge_low(items, [pltpu.roll(x, shift, 0) for x in items])
            for i in range(R):
                x = jnp.where(items[i] < 0.5 * BIG, items[i], 0.0)
                rows[which, i : i + 1, 256 * pair : 256 * pair + 128] = x[0:1]
                rows[which, i : i + 1, 256 * pair + 128 : 256 * pair + 256] = x[4:5]
        srows[which] = rows[which].astype(jnp.bfloat16)
        return carry

    def rows_copy(c, slot_r, which):
        return pltpu.make_async_remote_copy(
            src_ref=srows.at[which], dst_ref=drows.at[slot_r, which], send_sem=rs_sem.at[which, c],
            recv_sem=rr_sem.at[which, slot_r], device_id={"dom": c}, device_id_type=pl.DeviceIdType.MESH)

    for which in range(2):
        both(which, 0)

        def send_rows(o, carry):
            rows_copy(lax.rem(dom + o, doms), dom, which).start()
            return carry

        lax.fori_loop(1, doms, send_rows, 0)
    drows[dom] = srows[...]

    def take_rows(o, carry):
        s = lax.rem(dom + doms - o, doms)
        rows_copy(s, s, 0).wait_recv()
        rows_copy(s, s, 1).wait_recv()
        return carry

    lax.fori_loop(1, doms, take_rows, 0)
    moved = jnp.zeros((2 * R, per), jnp.float32)
    for d, pick in selections():
        moved = moved + dot_nt(jnp.concatenate([drows[d, 0], drows[d, 1]], axis=0), pick)
    out_rows[...] = moved.astype(jnp.bfloat16)

    def drain_pts(o, carry):
        c = lax.rem(me + o, n)
        info_copy(c, c, me).wait_send()
        vec_copy(c, c, me).wait_send()
        return carry

    def drain_dom(o, carry):
        c = lax.rem(dom + o, doms)
        dom_copy(c, dom, part, dpart, ps_sem, pr_sem).wait_send()
        dom_copy(c, dom, own_ref, dvec, ds_sem, dr_sem).wait_send()
        rows_copy(c, dom, 0).wait_send()
        rows_copy(c, dom, 1).wait_send()
        return carry

    lax.fori_loop(1, n, drain_pts, 0)
    lax.fori_loop(1, doms, drain_dom, 0)


def place(found_vec, found_rows, out_vec, out_rev, out_join):
    out_vec[...] = found_vec[...]
    out_rev[...] = found_rows[:R]
    out_join[...] = found_rows[R:]


def solution(mesh):
    n, doms = mesh.shape["pts"], mesh.shape["dom"]

    def per_device(vectors, neighbor_shards, neighbor_locals, partition):
        per, depth = vectors.shape[1:]
        width = neighbor_shards.shape[2]
        list_len = neighbor_locals.shape[2]
        cap = per // 8
        lanes = (cap // 8) * list_len
        operands = [vectors[0], neighbor_shards[0].T, neighbor_locals[0].T, partition]
        if width > 1:
            operands.append(neighbor_shards[0].T[jnp.arange(list_len) % width])
        bf16, f32, i32 = jnp.bfloat16, jnp.float32, jnp.int32
        dma = pltpu.SemaphoreType.DMA
        vmem = pl.BlockSpec(memory_space=pltpu.VMEM)
        anywhere = pl.BlockSpec(memory_space=pltpu.HBM)
        shapes = (jax.ShapeDtypeStruct((per, depth), bf16), jax.ShapeDtypeStruct((2 * R, per), bf16))
        found_vec, found_rows = pl.pallas_call(
            functools.partial(kernel, n, doms, cap),
            out_shape=shapes,
            in_specs=[anywhere] * len(operands),
            out_specs=(vmem, vmem),
            scratch_shapes=[
                pltpu.VMEM((per, depth), bf16),
                pltpu.VMEM((width, per), i32),
                pltpu.VMEM((list_len, per), i32),
                pltpu.VMEM((1, per), i32),
                pltpu.VMEM((list_len, per), i32),
                pltpu.VMEM((n, cap, depth), bf16),
                pltpu.VMEM((n, 8, lanes), bf16),
                pltpu.VMEM((n, cap, depth), bf16),
                pltpu.VMEM((n, 8, lanes), bf16),
                pltpu.VMEM((doms, per, depth), bf16),
                pltpu.VMEM((doms, 1, per), i32),
                pltpu.VMEM((n, per), f32),
                pltpu.VMEM((per, lanes), bf16),
                pltpu.VMEM((per, lanes), f32),
                pltpu.VMEM((cap, 128), f32),
                pltpu.VMEM((8, per), f32),
                pltpu.VMEM((2, n, cap, per), bf16),
                pltpu.VMEM((per // 128, R, 8, 128), f32),
                pltpu.VMEM((2, R, per), f32),
                pltpu.VMEM((2, R, per), bf16),
                pltpu.VMEM((doms, 2, R, per), bf16),
                dma((5,)),
                dma((n,)), dma((n,)), dma((n,)), dma((n,)),
                dma((doms,)), dma((doms,)), dma((doms,)), dma((doms,)), dma((2, doms)), dma((2, doms)),
            ],
            compiler_params=pltpu.CompilerParams(
                collective_id=0, has_side_effects=True, vmem_limit_bytes=32 * 1024 * 1024),
        )(*[pltpu.with_memory_space_constraint(x, pltpu.HBM) for x in operands])
        out_vec, out_rev, out_join = pl.pallas_call(
            place,
            out_shape=(shapes[0], jax.ShapeDtypeStruct((R, per), bf16), jax.ShapeDtypeStruct((R, per), bf16)),
            in_specs=[vmem, vmem],
            out_specs=(vmem, vmem, vmem),
            compiler_params=pltpu.CompilerParams(vmem_limit_bytes=8 * 1024 * 1024),
        )(found_vec, found_rows)
        return out_vec[None], out_rev.T[None], out_join.T[None]

    return jax.shard_map(
        per_device,
        mesh=mesh,
        in_specs=(
            P("dom", "pts", None),
            P("dom", "pts", None),
            P("dom", "pts", None),
            P("dom", "pts"),
        ),
        out_specs=(P("dom", "pts", None), P("dom", "pts", None), P("dom", "pts", None)),
        check_vma=False,
    )
```
